256 devices in a mesh: section: 64 (over y, z, core), dp: 4 (over x).
Axes of the slice: x: 4, y: 4, z: 8, core: 2. Of those that a mesh axis runs over, the one named last changes fastest.
Arguments:
- tokens: bfloat16 [1024, 8192], P(('section', 'dp')), may hold values from -6 to 6
- norm_gain: float32 [8192], replicated, may hold values from 0.1 to 1.9
- gate_weight: bfloat16 [8192, 28672], P('dp', 'section'), may hold values from -0.0625 to 0.0625
- up_weight: bfloat16 [8192, 28672], P('dp', 'section'), may hold values from -0.0625 to 0.0625
- down_weight: bfloat16 [28672, 8192], P('section', 'dp'), may hold values from -0.03125 to 0.03125
Outputs:
- mixed: bfloat16 [1024, 8192], P(('section', 'dp'))
The draws below stay inside these ranges and needn't reach their ends.
All inputs are finite; a program needn't handle non-finite values.
Results may differ from the reference program's by a relative error of at most 0.0046.
Values may be sent and summed in bfloat16 or wider, within the bound.
No kernel may reach another device: no remote copies, remote signals or barrier semaphores. Data moves between devices by JAX's collectives and lax.ppermute only.
A program may use at most 128 MiB of HBM per device.

```python
import jax
import jax.numpy as jnp
from jax import lax

D = 8192
FF = 28672
TOKENS = 1024


def level_of(own_key, extent, pieces, least, high):
    def one(dim, blocks):
        draws = jax.random.uniform(jax.random.fold_in(jax.random.fold_in(own_key, 6), dim), (blocks,), jnp.float32, least / len(pieces), high / len(pieces))
        return jnp.repeat(jnp.exp(draws), extent[dim] // blocks).reshape((-1,) + (1,) * (len(extent) - dim - 1))

    loudness = one(*pieces[0])
    for cut in pieces[1:]:
        loudness = loudness * one(*cut)
    return loudness


def noise(rng, extent, scale, reach, split=(), held_as=jnp.bfloat16):
    values = jax.random.normal(rng, extent, jnp.float32) * scale
    if len(split) > 0:
        values = level_of(rng, extent, split, -0.22, 0.18) * values
    return jnp.clip(values, min=-reach, max=reach).astype(held_as)


def setup_inputs(seed: int = 0) -> dict:
    arg_keys = jax.random.split(jax.random.key(seed), 6)
    return {
        "tokens": noise(arg_keys[0], (TOKENS, D), 1.0, 6.0, ((0, 256),)),
        "norm_gain": jnp.clip(1.0 + 0.18 * jax.random.normal(arg_keys[1], (D,), jnp.float32), 0.1, 1.9),
        "gate_weight": noise(arg_keys[2], (D, FF), D ** -0.5, 0.0625, ((0, 4), (1, 64))),
        "up_weight": noise(arg_keys[3], (D, FF), D ** -0.5, 0.0625, ((0, 4), (1, 64))),
        "down_weight": noise(arg_keys[4], (FF, D), FF ** -0.5, 0.03125, ((0, 64), (1, 4))),
    }


def reference(tokens, norm_gain, gate_weight, up_weight, down_weight):
    wide = tokens.astype(jnp.float32)
    meansq = lax.optimization_barrier(jnp.mean(wide * wide, axis=1, keepdims=True))
    normed = (wide * jax.lax.rsqrt(meansq + 1e-05) * norm_gain[None, :]).astype(jnp.bfloat16)
    gate = jnp.dot(normed, gate_weight, preferred_element_type=jnp.float32)
    up = jnp.dot(normed, up_weight, preferred_element_type=jnp.float32)
    hidden = (jax.nn.silu(gate) * up).astype(jnp.bfloat16)
    summed = jnp.dot(hidden, down_weight, preferred_element_type=jnp.float32)
    return (wide + summed).astype(jnp.bfloat16)
```

```python
import jax
import jax.numpy as jnp
from jax import lax
from jax.sharding import Mesh
from jax.sharding import PartitionSpec as P

F32, BF16 = jnp.float32, jnp.bfloat16
SIZES = {"y": 4, "z": 8, "c": 2, "x": 4}


def shift(value, axis, step):
    n = SIZES[axis]
    return lax.ppermute(value, axis, [(i, (i + step) % n) for i in range(n)])


def rolled(blocks, start):
    return lax.dynamic_slice_in_dim(
        jnp.concatenate([blocks, blocks], axis=0), start, blocks.shape[0], axis=0
    )


def gather_z(block):
    half = block.shape[0] // 2
    from_low, from_high = [block], [block]
    for _ in range(3):
        from_low.append(shift(from_low[-1], "z", 1))
        from_high.append(shift(from_high[-1], "z", -1))
    far = jnp.concatenate(
        [shift(from_low[3][:half], "z", 1), shift(from_high[3][half:], "z", -1)], axis=0
    )
    return from_low + [far] + from_high[:0:-1]


def scatter_z(sums):
    pieces = [sums[:, 4 * k : 4 * k + 4] for k in range(8)]
    total = pieces[0]
    for k in (4, 3, 5, 2, 6, 1, 7):
        total = total + shift(pieces[k].astype(BF16), "z", -k).astype(F32)
    return total


def local(tokens, norm_gain, gate_weight, up_weight, down_weight):
    x = lax.axis_index("x")
    gate_t, up_t = gate_weight.T, up_weight.T
    first = jnp.concatenate(
        [gate_t, shift(gate_t, "c", 1), up_t, shift(up_t, "c", 1)], axis=0
    )
    second = jnp.concatenate([down_weight, shift(down_weight, "c", 1)], axis=0)
    hidden_units = second.shape[0]
    rows, width = tokens.shape
    part = width // 4

    wide = tokens.astype(F32)
    mean_square = jnp.mean(wide * wide, axis=1, keepdims=True)
    normed = (wide * lax.rsqrt(mean_square + 1e-05) * norm_gain[None, :]).astype(BF16)
    blocks = rolled(normed.reshape(rows, 4, part).transpose(1, 0, 2), x)
    own = jnp.stack(
        [blocks[0]] + [shift(blocks[4 - r], "x", 4 - r) for r in (1, 2, 3)]
    )

    plane = jnp.concatenate(gather_z(own), axis=1)
    planes = [plane] + [shift(plane, "y", k) for k in (1, 2, 3)]

    many = jnp.concatenate(planes, axis=1)
    partial = lax.dot_general(
        many.reshape(-1, part), first, (((1,), (1,)), ((), ())), preferred_element_type=F32
    ).reshape(4, -1, 2 * hidden_units)
    both = partial[0]
    for k in (2, 1, 3):
        both = both + shift(partial[k].astype(BF16), "x", k).astype(F32)
    hidden = (jax.nn.silu(both[:, :hidden_units]) * both[:, hidden_units:]).astype(BF16)
    all_hidden = jnp.concatenate([hidden] + [shift(hidden, "x", -k) for k in (1, 2, 3)], axis=0)
    down = lax.dot_general(
        all_hidden, second, (((1,), (0,)), ((), ())), preferred_element_type=F32
    ).reshape(4, 4, -1, part)

    summed = down[:, 0]
    for k in (2, 1, 3):
        summed = summed + shift(down[:, k].astype(BF16), "y", -k).astype(F32)
    mine = scatter_z(summed)
    columns = jnp.stack([mine[0]] + [shift(mine[4 - r], "x", 4 - r) for r in (1, 2, 3)])
    ordered = rolled(columns, (4 - x) % 4).transpose(1, 0, 2).reshape(rows, width)
    return (wide + ordered).astype(BF16)


def solution(mesh):
    torus = Mesh(mesh.devices.reshape(4, 8, 2, 4), ("y", "z", "c", "x"))
    section = ("y", "z", "c")
    return jax.shard_map(
        local,
        mesh=torus,
        in_specs=(
            P(section + ("x",), None),
            P(),
            P("x", section),
            P("x", section),
            P(section, "x"),
        ),
        out_specs=P(section + ("x",), None),
        check_vma=False,
    )
```

```python
import jax
import jax.numpy as jnp
from jax import lax
from jax.sharding import Mesh
from jax.sharding import PartitionSpec as P

F32, BF16 = jnp.float32, jnp.bfloat16
SIZES = {"y": 4, "z": 8, "c": 2, "x": 4}


def shift(value, axis, step):
    n = SIZES[axis]
    return lax.ppermute(value, axis, [(i, (i + step) % n) for i in range(n)])


def along_z(value, first, second):
    steps = (first, second)
    pairs = [
        (2 * z + c, 2 * ((z + steps[c]) % 8) + c) for z in range(8) for c in range(2)
    ]
    return lax.ppermute(value, ("z", "c"), pairs)


def rolled(blocks, start):
    return lax.dynamic_slice_in_dim(
        jnp.concatenate([blocks, blocks], axis=0), start, blocks.shape[0], axis=0
    )


def together(*values):
    return lax.optimization_barrier(values)


def gather_z(pair):
    near = along_z(pair, 1, -1)
    base = along_z(pair, 0, 4)
    far = along_z(jnp.concatenate([pair, near], axis=1), 2, -2)
    return jnp.concatenate([base, near, far], axis=1)


def scatter_z(sums):
    n = sums.shape[1] // 4
    far = along_z(sums[:, 2 * n :].astype(BF16), -2, 2).astype(F32)
    base = along_z(sums[:, :n].astype(BF16), 0, 4).astype(F32)
    near = along_z((sums[:, n : 2 * n] + far[:, n:]).astype(BF16), -1, 1).astype(F32)
    return base + far[:, :n] + near


def local(tokens, norm_gain, gate_weight, up_weight, down_weight):
    x, core = lax.axis_index("x"), lax.axis_index("c")
    gate_t, up_t = gate_weight.T, up_weight.T
    first = [gate_t, shift(gate_t, "c", 1), up_t, shift(up_t, "c", 1)]
    second = jnp.concatenate([down_weight, shift(down_weight, "c", 1)], axis=0)
    units = second.shape[0]
    rows, width = tokens.shape
    part = width // 4

    wide = tokens.astype(F32)
    mean_square = jnp.mean(wide * wide, axis=1, keepdims=True)
    normed = (wide * lax.rsqrt(mean_square + 1e-05) * norm_gain[None, :]).astype(BF16)
    blocks = rolled(normed.reshape(rows, 4, part).transpose(1, 0, 2), x)
    own = jnp.stack(
        [blocks[0]] + [shift(blocks[4 - r], "x", 4 - r) for r in (1, 2, 3)]
    )
    plane = gather_z(lax.all_gather(own, "c", axis=1, tiled=True))
    tall = plane.shape[1]
    *first, own_plane = together(*first, plane)
    first = jnp.concatenate(first, axis=0)

    def project(block):
        return lax.dot_general(
            block.reshape(-1, part), first, (((1,), (1,)), ((), ())), preferred_element_type=F32
        ).reshape(4, -1, 2 * units)

    def exchange(partial):
        return [shift(partial[k].astype(BF16), "x", k) for k in (2, 1, 3)]

    def activate(both, received):
        for value in received:
            both = both + value.astype(F32)
        return (jax.nn.silu(both[:, :units]) * both[:, units:]).astype(BF16)

    def spread(hidden):
        return [shift(hidden, "x", -k) for k in (1, 2, 3)]

    def down(everyone):
        return lax.dot_general(
            jnp.concatenate(everyone, axis=0),
            second,
            (((1,), (0,)), ((), ())),
            preferred_element_type=F32,
        ).reshape(4, -1, part)

    behind, ahead, opposite = (shift(plane, "y", k) for k in (1, 3, 2))
    own_partial = project(own_plane)
    own_sums = exchange(own_partial)
    own_kept, behind, ahead = together(own_partial[0], behind, ahead)

    side_partial = project(jnp.concatenate([behind, ahead], axis=1))
    side_sums = exchange(side_partial)
    side_kept, *own_sums = together(side_partial[0], *own_sums)
    own_hidden = activate(own_kept, own_sums)
    own_spread = spread(own_hidden)
    own_hidden, opposite = together(own_hidden, opposite)

    far_partial = project(opposite)
    far_sums = exchange(far_partial)
    far_kept, *side_sums = together(far_partial[0], *side_sums)
    side_hidden = activate(side_kept, side_sums)
    side_spread = spread(side_hidden)
    side_hidden, *far_sums = together(side_hidden, *far_sums)
    far_hidden = activate(far_kept, far_sums)
    far_spread = spread(far_hidden)

    own_down = down([own_hidden] + own_spread)
    side_down = down([side_hidden] + side_spread)
    far_down = down([far_hidden] + far_spread)
    summed = own_down
    for value, k in ((side_down[:, :tall], -1), (side_down[:, tall:], -3), (far_down, -2)):
        summed = summed + shift(value.astype(BF16), "y", k).astype(F32)

    pair = scatter_z(summed)
    low, high = pair[:, :rows], pair[:, rows:]
    mine = jnp.where(core == 0, low, high)
    other = jnp.where(core == 0, high, low).astype(BF16)
    mine = mine + shift(other, "c", 1).astype(F32)
    columns = [mine[0]] + [shift(mine[k], "x", k) for k in (1, 2, 3)]
    ordered = [columns[0]] * 4
    for k in (1, 2, 3):
        ordered = [
            jnp.where((x - block) % 4 == k, columns[k], value)
            for block, value in enumerate(ordered)
        ]
    return (wide + jnp.concatenate(ordered, axis=1)).astype(BF16)


def solution(mesh):
    torus = Mesh(mesh.devices.reshape(4, 8, 2, 4), ("y", "z", "c", "x"))
    section = ("y", "z", "c")
    return jax.shard_map(
        local,
        mesh=torus,
        in_specs=(
            P(section + ("x",), None),
            P(),
            P("x", section),
            P("x", section),
            P(section, "x"),
        ),
        out_specs=P(section + ("x",), None),
        check_vma=False,
    )
```

```python
import jax
import jax.numpy as jnp
from jax import lax
from jax.sharding import Mesh
from jax.sharding import PartitionSpec as P

F32, BF16 = jnp.float32, jnp.bfloat16
SIZES = {"y": 4, "z": 8, "c": 2, "x": 4}


def shift(value, axis, step):
    n = SIZES[axis]
    return lax.ppermute(value, axis, [(i, (i + step) % n) for i in range(n)])


def along_z(value, first, second):
    steps = (first, second)
    pairs = [
        (2 * z + c, 2 * ((z + steps[c]) % 8) + c) for z in range(8) for c in range(2)
    ]
    return lax.ppermute(value, ("z", "c"), pairs)


def rolled(blocks, start):
    return lax.dynamic_slice_in_dim(
        jnp.concatenate([blocks, blocks], axis=0), start, blocks.shape[0], axis=0
    )


def together(*values):
    return lax.optimization_barrier(values)


def local(tokens, norm_gain, gate_weight, up_weight, down_weight):
    x, core = lax.axis_index("x"), lax.axis_index("c")
    gate_t, up_t = gate_weight.T, up_weight.T
    first = [gate_t, shift(gate_t, "c", 1), up_t, shift(up_t, "c", 1)]
    second = jnp.concatenate([down_weight, shift(down_weight, "c", 1)], axis=0)
    units = second.shape[0]
    rows, width = tokens.shape
    part = width // 4

    wide = tokens.astype(F32)
    mean_square = jnp.mean(wide * wide, axis=1, keepdims=True)
    normed = (wide * lax.rsqrt(mean_square + 1e-05) * norm_gain[None, :]).astype(BF16)
    blocks = rolled(normed.reshape(rows, 4, part).transpose(1, 0, 2), x)
    own = jnp.stack(
        [blocks[0]] + [shift(blocks[4 - r], "x", 4 - r) for r in (1, 2, 3)]
    )
    pair = lax.all_gather(own, "c", axis=1, tiled=True)
    near, base = along_z(pair, 1, -1), along_z(pair, 0, 4)
    far = along_z(jnp.concatenate([pair, near], axis=1), 2, -2)
    near = jnp.concatenate([base, near], axis=1)

    def project(block):
        return lax.dot_general(
            block.reshape(-1, part), first, (((1,), (1,)), ((), ())), preferred_element_type=F32
        ).reshape(4, -1, 2 * units)

    def exchange(partial):
        return [shift(partial[k].astype(BF16), "x", k) for k in (2, 1, 3)]

    def activate(both, received):
        for value in received:
            both = both + value.astype(F32)
        return (jax.nn.silu(both[:, :units]) * both[:, units:]).astype(BF16)

    def spread(hidden):
        return [shift(hidden, "x", -k) for k in (1, 2, 3)]

    def down(everyone):
        return lax.dot_general(
            jnp.concatenate(everyone, axis=0),
            second,
            (((1,), (0,)), ((), ())),
            preferred_element_type=F32,
        ).reshape(4, -1, part)

    def sum_over_y(blocks, received):
        return sum((value.astype(F32) for value in received), blocks[0])

    def over_y(value):
        return [shift(value, "y", k) for k in (1, 3, 2)]

    def back_over_y(blocks):
        return [shift(blocks[k].astype(BF16), "y", -k) for k in (1, 3, 2)]

    def by_y(value):
        return [value[:, k * slots : (k + 1) * slots] for k in range(4)]

    slots = near.shape[1]
    near_y = over_y(near)
    *first, far_own = together(*first, far)
    first = jnp.concatenate(first, axis=0)
    far_y = over_y(far)

    first, near_1, near_3, near_2 = together(first, *near_y)
    near_partial = project(jnp.concatenate([near, near_1, near_2, near_3], axis=1))
    near_sums = exchange(near_partial)
    near_hidden = activate(near_partial[0], near_sums)
    near_spread = spread(near_hidden)

    near_hidden, far_1, far_3, far_2 = together(near_hidden, *far_y)
    far_partial = project(jnp.concatenate([far_own, far_1, far_2, far_3], axis=1))
    far_sums = exchange(far_partial)
    far_kept, *near_spread = together(far_partial[0], *near_spread)

    near_down = by_y(down([near_hidden] + near_spread))
    near_back = back_over_y(near_down)
    near_down[0], *far_sums = together(near_down[0], *far_sums)
    far_hidden = activate(far_kept, far_sums)
    far_spread = spread(far_hidden)
    far_hidden, *near_back = together(far_hidden, *near_back)

    near_total = sum_over_y(near_down, near_back)
    half = slots // 2
    near_pieces = [
        along_z(near_total[:, half:].astype(BF16), -1, 1),
        along_z(near_total[:, :half].astype(BF16), 0, 4),
    ]
    far_down = by_y(down([far_hidden] + far_spread))
    far_back = back_over_y(far_down)
    *near_pieces, back_1, back_3, back_2 = together(*near_pieces, *far_back)
    far_total = sum_over_y(far_down, (back_1, back_3, back_2))
    far_pieces = [
        along_z(far_total[:, half:].astype(BF16), -3, 3),
        along_z(far_total[:, :half].astype(BF16), -2, 2),
    ]
    pair = sum(piece.astype(F32) for piece in near_pieces + far_pieces)
    low, high = pair[:, :rows], pair[:, rows:]
    mine = jnp.where(core == 0, low, high)
    other = jnp.where(core == 0, high, low).astype(BF16)
    mine = mine + shift(other, "c", 1).astype(F32)
    columns = [mine[0]] + [shift(mine[k], "x", k) for k in (1, 2, 3)]
    ordered = [columns[0]] * 4
    for k in (1, 2, 3):
        ordered = [
            jnp.where((x - block) % 4 == k, columns[k], value)
            for block, value in enumerate(ordered)
        ]
    return (wide + jnp.concatenate(ordered, axis=1)).astype(BF16)


def solution(mesh):
    torus = Mesh(mesh.devices.reshape(4, 8, 2, 4), ("y", "z", "c", "x"))
    section = ("y", "z", "c")
    return jax.shard_map(
        local,
        mesh=torus,
        in_specs=(
            P(section + ("x",), None),
            P(),
            P("x", section),
            P("x", section),
            P(section, "x"),
        ),
        out_specs=P(section + ("x",), None),
        check_vma=False,
    )
```

```python
import jax
import jax.numpy as jnp
from jax import lax
from jax.sharding import Mesh
from jax.sharding import PartitionSpec as P

F32, BF16 = jnp.float32, jnp.bfloat16
SIZES = {"y": 4, "z": 8, "c": 2, "x": 4}


def shift(value, axis, step):
    n = SIZES[axis]
    return lax.ppermute(value, axis, [(i, (i + step) % n) for i in range(n)])


def along_z(value, first, second):
    steps = (first, second)
    pairs = [
        (2 * z + c, 2 * ((z + steps[c]) % 8) + c) for z in range(8) for c in range(2)
    ]
    return lax.ppermute(value, ("z", "c"), pairs)


def rolled(blocks, start):
    return lax.dynamic_slice_in_dim(
        jnp.concatenate([blocks, blocks], axis=0), start, blocks.shape[0], axis=0
    )


def together(*values):
    return lax.optimization_barrier(values)


def local(tokens, norm_gain, gate_weight, up_weight, down_weight):
    x, core = lax.axis_index("x"), lax.axis_index("c")
    gate_t, up_t = gate_weight.T, up_weight.T
    first = [gate_t, shift(gate_t, "c", 1), up_t, shift(up_t, "c", 1)]
    second = [down_weight, shift(down_weight, "c", 1)]
    units = 2 * down_weight.shape[0]
    rows, width = tokens.shape
    part = width // 4

    wide = tokens.astype(F32)
    mean_square = jnp.mean(wide * wide, axis=1, keepdims=True)
    normed = (wide * lax.rsqrt(mean_square + 1e-05) * norm_gain[None, :]).astype(BF16)
    blocks = rolled(normed.reshape(rows, 4, part).transpose(1, 0, 2), x)
    own = jnp.stack(
        [blocks[0]] + [shift(blocks[4 - r], "x", 4 - r) for r in (1, 2, 3)]
    )
    pair = lax.all_gather(own, "c", axis=1, tiled=True)
    near, base = along_z(pair, 1, -1), along_z(pair, 0, 4)
    far = along_z(jnp.concatenate([pair, near], axis=1), 2, -2)
    near = jnp.concatenate([base, near], axis=1)

    def project(weights, block):
        return lax.dot_general(
            block.reshape(-1, part), weights, (((1,), (1,)), ((), ())), preferred_element_type=F32
        ).reshape(4, -1, 2 * units)

    def exchange(partial):
        return [shift(partial[k].astype(BF16), "x", k) for k in (2, 1, 3)]

    def activate(both, received):
        for value in received:
            both = both + value.astype(F32)
        return (jax.nn.silu(both[:, :units]) * both[:, units:]).astype(BF16)

    def spread(hidden):
        return [shift(hidden, "x", -k) for k in (1, 2, 3)]

    def down(weights, everyone):
        return lax.dot_general(
            jnp.concatenate(everyone, axis=0),
            weights,
            (((1,), (0,)), ((), ())),
            preferred_element_type=F32,
        ).reshape(4, -1, part)

    def sum_over_y(blocks, received):
        return sum((value.astype(F32) for value in received), blocks[0])

    def over_y(value):
        return [shift(value, "y", k) for k in (1, 3, 2)]

    def back_over_y(blocks):
        return [shift(blocks[k].astype(BF16), "y", -k) for k in (1, 3, 2)]

    def by_y(value):
        return [value[:, k * slots : (k + 1) * slots] for k in range(4)]

    slots = near.shape[1]
    near_y = over_y(near)
    *first, near_own = together(*first, near)
    first, far = together(jnp.concatenate(first, axis=0), far)
    far_y = over_y(far)
    *second, far_own = together(*second, far)
    second = jnp.concatenate(second, axis=0)

    first, second, near_1, near_3, near_2 = together(first, second, *near_y)
    near_partial = project(first, jnp.concatenate([near_own, near_1, near_2, near_3], axis=1))
    near_sums = exchange(near_partial)
    near_hidden = activate(near_partial[0], near_sums)
    near_spread = spread(near_hidden)

    near_hidden, far_1, far_3, far_2 = together(near_hidden, *far_y)
    far_partial = project(first, jnp.concatenate([far_own, far_1, far_2, far_3], axis=1))
    far_sums = exchange(far_partial)
    far_kept, *near_spread = together(far_partial[0], *near_spread)

    near_down = by_y(down(second, [near_hidden] + near_spread))
    near_back = back_over_y(near_down)
    near_down[0], *far_sums = together(near_down[0], *far_sums)
    far_hidden = activate(far_kept, far_sums)
    far_spread = spread(far_hidden)
    far_hidden, *near_back = together(far_hidden, *near_back)

    near_total = sum_over_y(near_down, near_back)
    half = slots // 2
    near_pieces = [
        along_z(near_total[:, half:].astype(BF16), -1, 1),
        along_z(near_total[:, :half].astype(BF16), 0, 4),
    ]
    far_down = by_y(down(second, [far_hidden] + far_spread))
    far_back = back_over_y(far_down)
    *near_pieces, back_1, back_3, back_2 = together(*near_pieces, *far_back)
    far_total = sum_over_y(far_down, (back_1, back_3, back_2))
    far_pieces = [
        along_z(far_total[:, half:].astype(BF16), -3, 3),
        along_z(far_total[:, :half].astype(BF16), -2, 2),
    ]
    pair = sum(piece.astype(F32) for piece in near_pieces + far_pieces)
    low, high = pair[:, :rows], pair[:, rows:]
    mine = jnp.where(core == 0, low, high)
    other = jnp.where(core == 0, high, low).astype(BF16)
    mine = mine + shift(other, "c", 1).astype(F32)
    columns = [mine[0]] + [shift(mine[k], "x", k) for k in (1, 2, 3)]
    ordered = [columns[0]] * 4
    for k in (1, 2, 3):
        ordered = [
            jnp.where((x - block) % 4 == k, columns[k], value)
            for block, value in enumerate(ordered)
        ]
    return (wide + jnp.concatenate(ordered, axis=1)).astype(BF16)


def solution(mesh):
    torus = Mesh(mesh.devices.reshape(4, 8, 2, 4), ("y", "z", "c", "x"))
    section = ("y", "z", "c")
    return jax.shard_map(
        local,
        mesh=torus,
        in_specs=(
            P(section + ("x",), None),
            P(),
            P("x", section),
            P("x", section),
            P(section, "x"),
        ),
        out_specs=P(section + ("x",), None),
        check_vma=False,
    )
```

```python
import jax
import jax.numpy as jnp
from jax import lax
from jax.sharding import Mesh
from jax.sharding import PartitionSpec as P

F32, BF16 = jnp.float32, jnp.bfloat16
SIZES = {"y": 4, "z": 8, "c": 2, "x": 4}


def shift(value, axis, step):
    n = SIZES[axis]
    return lax.ppermute(value, axis, [(i, (i + step) % n) for i in range(n)])


def along_z(value, first, second):
    steps = (first, second)
    pairs = [
        (2 * z + c, 2 * ((z + steps[c]) % 8) + c) for z in range(8) for c in range(2)
    ]
    return lax.ppermute(value, ("z", "c"), pairs)


def rolled(blocks, start):
    return lax.dynamic_slice_in_dim(
        jnp.concatenate([blocks, blocks], axis=0), start, blocks.shape[0], axis=0
    )


def together(*values):
    return lax.optimization_barrier(values)


def local(tokens, norm_gain, gate_weight, up_weight, down_weight):
    x, core = lax.axis_index("x"), lax.axis_index("c")
    gate_t, up_t = gate_weight.T, up_weight.T
    first = [gate_t, shift(gate_t, "c", 1), up_t, shift(up_t, "c", 1)]
    second = [down_weight, shift(down_weight, "c", 1)]
    units = 2 * down_weight.shape[0]
    rows, width = tokens.shape
    part = width // 4

    wide = tokens.astype(F32)
    mean_square = jnp.mean(wide * wide, axis=1, keepdims=True)
    normed = (wide * lax.rsqrt(mean_square + 1e-05) * norm_gain[None, :]).astype(BF16)
    blocks = rolled(normed.reshape(rows, 4, part).transpose(1, 0, 2), x)
    own = jnp.stack(
        [blocks[0]] + [shift(blocks[4 - r], "x", 4 - r) for r in (1, 2, 3)]
    )
    opposite = along_z(own, 4, 4)
    pair = lax.all_gather(own, "c", axis=1, tiled=True)
    near = along_z(pair, 1, -1)
    far = along_z(jnp.concatenate([pair, near], axis=1), 2, -2)
    near = jnp.concatenate([own, opposite, near], axis=1)

    def project(weights, block):
        return lax.dot_general(
            block.reshape(-1, part), weights, (((1,), (1,)), ((), ())), preferred_element_type=F32
        ).reshape(4, -1, 2 * units)

    def exchange(partial):
        return [shift(partial[k].astype(BF16), "x", k) for k in (2, 1, 3)]

    def activate(both, received):
        for value in received:
            both = both + value.astype(F32)
        return (jax.nn.silu(both[:, :units]) * both[:, units:]).astype(BF16)

    def spread(hidden):
        return [shift(hidden, "x", -k) for k in (1, 2, 3)]

    def down(weights, everyone):
        return lax.dot_general(
            jnp.concatenate(everyone, axis=0),
            weights,
            (((1,), (0,)), ((), ())),
            preferred_element_type=F32,
        ).reshape(4, -1, part)

    def sum_over_y(blocks, received):
        return sum((value.astype(F32) for value in received), blocks[0])

    def over_y(value):
        return [shift(value, "y", k) for k in (1, 3, 2)]

    def back_over_y(blocks):
        return [shift(blocks[k].astype(BF16), "y", -k) for k in (1, 3, 2)]

    def by_y(value):
        return [value[:, k * slots : (k + 1) * slots] for k in range(4)]

    slots = near.shape[1]
    near_y = over_y(near)
    *first, near_own = together(*first, near)
    first, far = together(jnp.concatenate(first, axis=0), far)
    far_y = over_y(far)

    first, near_1, near_3, near_2 = together(first, *near_y)
    near_partial = project(first, jnp.concatenate([near_own, near_1, near_2, near_3], axis=1))
    near_sums = exchange(near_partial)
    *second, near_kept = together(*second, near_partial[0])
    second = jnp.concatenate(second, axis=0)

    second, far_1, far_3, far_2 = together(second, *far_y)
    far_partial = project(first, jnp.concatenate([far, far_1, far_2, far_3], axis=1))
    far_sums = exchange(far_partial)
    far_kept, *near_sums = together(far_partial[0], *near_sums)
    near_hidden = activate(near_kept, near_sums)
    near_spread = spread(near_hidden)

    near_down = by_y(down(second, [near_hidden] + near_spread))
    near_back = back_over_y(near_down)
    near_down[0], *far_sums = together(near_down[0], *far_sums)
    far_hidden = activate(far_kept, far_sums)
    far_spread = spread(far_hidden)
    far_hidden, *near_back = together(far_hidden, *near_back)

    near_total = sum_over_y(near_down, near_back)
    near_pieces = [
        along_z(near_total[:, 2 * rows :].astype(BF16), -1, 1),
        along_z(near_total[:, rows : 2 * rows].astype(BF16), 4, 4),
    ]
    far_down = by_y(down(second, [far_hidden] + far_spread))
    far_back = back_over_y(far_down)
    *near_pieces, back_1, back_3, back_2 = together(*near_pieces, *far_back)
    far_total = sum_over_y(far_down, (back_1, back_3, back_2))
    pair = sum(
        piece.astype(F32)
        for piece in (
            near_pieces[0],
            along_z(far_total[:, 2 * rows :].astype(BF16), -3, 3),
            along_z(far_total[:, : 2 * rows].astype(BF16), -2, 2),
        )
    )
    low, high = pair[:, :rows], pair[:, rows:]
    mine = near_total[:, :rows] + near_pieces[1].astype(F32) + jnp.where(core == 0, low, high)
    other = jnp.where(core == 0, high, low).astype(BF16)
    mine = mine + shift(other, "c", 1).astype(F32)
    columns = [mine[0]] + [shift(mine[k], "x", k) for k in (1, 2, 3)]
    ordered = [columns[0]] * 4
    for k in (1, 2, 3):
        ordered = [
            jnp.where((x - block) % 4 == k, columns[k], value)
            for block, value in enumerate(ordered)
        ]
    return (wide + jnp.concatenate(ordered, axis=1)).astype(BF16)


def solution(mesh):
    torus = Mesh(mesh.devices.reshape(4, 8, 2, 4), ("y", "z", "c", "x"))
    section = ("y", "z", "c")
    return jax.shard_map(
        local,
        mesh=torus,
        in_specs=(
            P(section + ("x",), None),
            P(),
            P("x", section),
            P("x", section),
            P(section, "x"),
        ),
        out_specs=P(section + ("x",), None),
        check_vma=False,
    )
```

```python
import jax
import jax.numpy as jnp
from jax import lax
from jax.sharding import Mesh
from jax.sharding import PartitionSpec as P

F32, BF16 = jnp.float32, jnp.bfloat16
SIZES = {"y": 4, "z": 8, "c": 2, "x": 4}


def shift(value, axis, step):
    n = SIZES[axis]
    return lax.ppermute(value, axis, [(i, (i + step) % n) for i in range(n)])


def along_z(value, first, second):
    steps = (first, second)
    pairs = [
        (2 * z + c, 2 * ((z + steps[c]) % 8) + c) for z in range(8) for c in range(2)
    ]
    return lax.ppermute(value, ("z", "c"), pairs)


def rolled(blocks, start):
    return lax.dynamic_slice_in_dim(
        jnp.concatenate([blocks, blocks], axis=0), start, blocks.shape[0], axis=0
    )


def together(*values):
    return lax.optimization_barrier(values)


def local(tokens, norm_gain, gate_weight, up_weight, down_weight):
    x, core = lax.axis_index("x"), lax.axis_index("c")
    gate_t, up_t = gate_weight.T, up_weight.T
    first = [gate_t, shift(gate_t, "c", 1), up_t, shift(up_t, "c", 1)]
    second = [down_weight, shift(down_weight, "c", 1)]
    units = 2 * down_weight.shape[0]
    rows, width = tokens.shape
    part = width // 4

    wide = tokens.astype(F32)
    mean_square = jnp.mean(wide * wide, axis=1, keepdims=True)
    normed = (wide * lax.rsqrt(mean_square + 1e-05) * norm_gain[None, :]).astype(BF16)
    blocks = rolled(normed.reshape(rows, 4, part).transpose(1, 0, 2), x)
    own = jnp.stack(
        [blocks[0]] + [shift(blocks[4 - r], "x", 4 - r) for r in (1, 2, 3)]
    )
    opposite = along_z(own, 4, 4)
    pair = lax.all_gather(own, "c", axis=1, tiled=True)
    near = along_z(pair, 1, -1)
    far = along_z(jnp.concatenate([pair, near], axis=1), 2, -2)
    near = jnp.concatenate([own, opposite, near], axis=1)

    def project(weights, block):
        return lax.dot_general(
            block.reshape(-1, part), weights, (((1,), (1,)), ((), ())), preferred_element_type=F32
        ).reshape(4, -1, 2 * units)

    def exchange(partial):
        return [shift(partial[k].astype(BF16), "x", k) for k in (2, 1, 3)]

    def activate(both, received):
        for value in received:
            both = both + value.astype(F32)
        return (jax.nn.silu(both[:, :units]) * both[:, units:]).astype(BF16)

    def spread(hidden):
        return [shift(hidden, "x", -k) for k in (1, 2, 3)]

    def down(weights, everyone):
        return lax.dot_general(
            jnp.concatenate(everyone, axis=0),
            weights,
            (((1,), (0,)), ((), ())),
            preferred_element_type=F32,
        ).reshape(4, -1, part)

    def sum_over_y(blocks, received):
        return sum((value.astype(F32) for value in received), blocks[0])

    def over_y(value):
        return [shift(value, "y", k) for k in (1, 3, 2)]

    def back_over_y(blocks):
        return [shift(blocks[k].astype(BF16), "y", -k) for k in (1, 3, 2)]

    def by_y(value):
        return [value[:, k * slots : (k + 1) * slots] for k in range(4)]

    slots = near.shape[1]
    near_y = over_y(near)
    *first, near_own = together(*first, near)
    first, far = together(jnp.concatenate(first, axis=0), far)
    far_y = over_y(far)

    first, near_1, near_3, near_2 = together(first, *near_y)
    near_partial = project(first, jnp.concatenate([near_own, near_1, near_2, near_3], axis=1))
    near_sums = exchange(near_partial)
    *second, near_kept = together(*second, near_partial[0])
    second = jnp.concatenate(second, axis=0)

    second, far_1, far_3, far_2 = together(second, *far_y)
    far_partial = project(first, jnp.concatenate([far, far_1, far_2, far_3], axis=1))
    far_sums = exchange(far_partial)
    far_kept, *near_sums = together(far_partial[0], *near_sums)
    near_hidden = activate(near_kept, near_sums)
    near_spread = spread(near_hidden)

    near_hidden, *far_sums = together(near_hidden, *far_sums)
    far_hidden = activate(far_kept, far_sums)
    far_spread = spread(far_hidden)
    far_hidden, *near_spread = together(far_hidden, *near_spread)

    near_down = by_y(down(second, [near_hidden] + near_spread))
    near_back = back_over_y(near_down)
    near_down[0], *far_spread = together(near_down[0], *far_spread)
    far_down = by_y(down(second, [far_hidden] + far_spread))
    far_back = back_over_y(far_down)
    far_down[0], *near_back = together(far_down[0], *near_back)

    near_total = sum_over_y(near_down, near_back)
    near_pieces = [
        along_z(near_total[:, 2 * rows :].astype(BF16), -1, 1),
        along_z(near_total[:, rows : 2 * rows].astype(BF16), 4, 4),
    ]
    near_pieces[0], back_1, back_3, back_2 = together(near_pieces[0], *far_back)
    far_total = sum_over_y(far_down, (back_1, back_3, back_2))
    pair = sum(
        piece.astype(F32)
        for piece in (
            near_pieces[0],
            along_z(far_total[:, 2 * rows :].astype(BF16), -3, 3),
            along_z(far_total[:, : 2 * rows].astype(BF16), -2, 2),
        )
    )
    low, high = pair[:, :rows], pair[:, rows:]
    mine = near_total[:, :rows] + near_pieces[1].astype(F32) + jnp.where(core == 0, low, high)
    other = jnp.where(core == 0, high, low).astype(BF16)
    mine = mine + shift(other, "c", 1).astype(F32)
    columns = [mine[0]] + [shift(mine[k], "x", k) for k in (1, 2, 3)]
    ordered = [columns[0]] * 4
    for k in (1, 2, 3):
        ordered = [
            jnp.where((x - block) % 4 == k, columns[k], value)
            for block, value in enumerate(ordered)
        ]
    return (wide + jnp.concatenate(ordered, axis=1)).astype(BF16)


def solution(mesh):
    torus = Mesh(mesh.devices.reshape(4, 8, 2, 4), ("y", "z", "c", "x"))
    section = ("y", "z", "c")
    return jax.shard_map(
        local,
        mesh=torus,
        in_specs=(
            P(section + ("x",), None),
            P(),
            P("x", section),
            P("x", section),
            P(section, "x"),
        ),
        out_specs=P(section + ("x",), None),
        check_vma=False,
    )
```

```python
import jax
import jax.numpy as jnp
from jax import lax
from jax.sharding import Mesh
from jax.sharding import PartitionSpec as P

F32, BF16 = jnp.float32, jnp.bfloat16
SIZES = {"y": 4, "z": 8, "c": 2, "x": 4}


def shift(value, axis, step):
    n = SIZES[axis]
    return lax.ppermute(value, axis, [(i, (i + step) % n) for i in range(n)])


def along_z(value, first, second):
    steps = (first, second)
    pairs = [
        (2 * z + c, 2 * ((z + steps[c]) % 8) + c) for z in range(8) for c in range(2)
    ]
    return lax.ppermute(value, ("z", "c"), pairs)


def rolled(blocks, start):
    return lax.dynamic_slice_in_dim(
        jnp.concatenate([blocks, blocks], axis=0), start, blocks.shape[0], axis=0
    )


def together(*values):
    return lax.optimization_barrier(values)


def local(tokens, norm_gain, gate_weight, up_weight, down_weight):
    x, core = lax.axis_index("x"), lax.axis_index("c")
    gate_t, up_t = gate_weight.T, up_weight.T
    first = [gate_t, shift(gate_t, "c", 1), up_t, shift(up_t, "c", 1)]
    second = [down_weight, shift(down_weight, "c", 1)]
    units = 2 * down_weight.shape[0]
    rows, width = tokens.shape
    part = width // 4

    wide = tokens.astype(F32)
    mean_square = jnp.mean(wide * wide, axis=1, keepdims=True)
    normed = (wide * lax.rsqrt(mean_square + 1e-05) * norm_gain[None, :]).astype(BF16)
    blocks = rolled(normed.reshape(rows, 4, part).transpose(1, 0, 2), x)
    own = jnp.stack(
        [blocks[0]] + [shift(blocks[4 - r], "x", 4 - r) for r in (1, 2, 3)]
    )
    pair = lax.all_gather(own, "c", axis=1, tiled=True)
    near = jnp.concatenate([along_z(pair, 0, -2), along_z(pair, 1, -1)], axis=1)
    far = along_z(near, 2, -2)

    def project(weights, block):
        return lax.dot_general(
            block.reshape(-1, part), weights, (((1,), (1,)), ((), ())), preferred_element_type=F32
        ).reshape(4, -1, 2 * units)

    def exchange(partial):
        return [shift(partial[k].astype(BF16), "x", k) for k in (2, 1, 3)]

    def activate(both, received):
        for value in received:
            both = both + value.astype(F32)
        return (jax.nn.silu(both[:, :units]) * both[:, units:]).astype(BF16)

    def spread(hidden):
        return [shift(hidden, "x", -k) for k in (1, 2, 3)]

    def down(weights, everyone):
        return lax.dot_general(
            jnp.concatenate(everyone, axis=0),
            weights,
            (((1,), (0,)), ((), ())),
            preferred_element_type=F32,
        ).reshape(4, -1, part)

    def sum_over_y(blocks, received):
        return sum((value.astype(F32) for value in received), blocks[0])

    def over_y(value):
        return [shift(value, "y", k) for k in (1, 3, 2)]

    def back_over_y(blocks):
        return [shift(blocks[k].astype(BF16), "y", -k) for k in (1, 3, 2)]

    def by_y(value):
        return [value[:, k * slots : (k + 1) * slots] for k in range(4)]

    slots = near.shape[1]
    near_y = over_y(near)
    *first, near_own = together(*first, near)
    first, far = together(jnp.concatenate(first, axis=0), far)
    far_y = over_y(far)

    first, near_1, near_3, near_2 = together(first, *near_y)
    near_partial = project(first, jnp.concatenate([near_own, near_1, near_2, near_3], axis=1))
    near_sums = exchange(near_partial)
    *second, near_kept = together(*second, near_partial[0])
    second = jnp.concatenate(second, axis=0)

    second, far_1, far_3, far_2 = together(second, *far_y)
    far_partial = project(first, jnp.concatenate([far, far_1, far_2, far_3], axis=1))
    far_sums = exchange(far_partial)
    far_kept, *near_sums = together(far_partial[0], *near_sums)
    near_hidden = activate(near_kept, near_sums)
    near_spread = spread(near_hidden)

    near_hidden, *far_sums = together(near_hidden, *far_sums)
    far_hidden = activate(far_kept, far_sums)
    far_spread = spread(far_hidden)
    far_hidden, *near_spread = together(far_hidden, *near_spread)

    near_down = by_y(down(second, [near_hidden] + near_spread))
    near_back = back_over_y(near_down)
    near_down[0], *far_spread = together(near_down[0], *far_spread)
    far_down = by_y(down(second, [far_hidden] + far_spread))
    far_back = back_over_y(far_down)
    far_down[0], *near_back = together(far_down[0], *near_back)

    near_total = sum_over_y(near_down, near_back)
    half = 2 * rows
    near_pieces = [
        along_z(near_total[:, :half].astype(BF16), 0, 2),
        along_z(near_total[:, half:].astype(BF16), -1, 1),
    ]
    *near_pieces, back_1, back_3, back_2 = together(*near_pieces, *far_back)
    far_total = sum_over_y(far_down, (back_1, back_3, back_2))
    far_pieces = [
        along_z(far_total[:, :half].astype(BF16), -2, 4),
        along_z(far_total[:, half:].astype(BF16), -3, 3),
    ]
    pair = sum(piece.astype(F32) for piece in near_pieces + far_pieces)
    low, high = pair[:, :rows], pair[:, rows:]
    mine = jnp.where(core == 0, low, high)
    other = jnp.where(core == 0, high, low).astype(BF16)
    mine = mine + shift(other, "c", 1).astype(F32)
    columns = [mine[0]] + [shift(mine[k], "x", k) for k in (1, 2, 3)]
    ordered = [columns[0]] * 4
    for k in (1, 2, 3):
        ordered = [
            jnp.where((x - block) % 4 == k, columns[k], value)
            for block, value in enumerate(ordered)
        ]
    return (wide + jnp.concatenate(ordered, axis=1)).astype(BF16)


def solution(mesh):
    torus = Mesh(mesh.devices.reshape(4, 8, 2, 4), ("y", "z", "c", "x"))
    section = ("y", "z", "c")
    return jax.shard_map(
        local,
        mesh=torus,
        in_specs=(
            P(section + ("x",), None),
            P(),
            P("x", section),
            P("x", section),
            P(section, "x"),
        ),
        out_specs=P(section + ("x",), None),
        check_vma=False,
    )
```

```python
import jax
import jax.numpy as jnp
from jax import lax
from jax.sharding import Mesh
from jax.sharding import PartitionSpec as P

F32, BF16 = jnp.float32, jnp.bfloat16
SIZES = {"y": 4, "z": 8, "c": 2, "x": 4}


def shift(value, axis, step):
    n = SIZES[axis]
    return lax.ppermute(value, axis, [(i, (i + step) % n) for i in range(n)])


def along_z(value, first, second):
    steps = (first, second)
    pairs = [
        (2 * z + c, 2 * ((z + steps[c]) % 8) + c) for z in range(8) for c in range(2)
    ]
    return lax.ppermute(value, ("z", "c"), pairs)


def rolled(blocks, start):
    return lax.dynamic_slice_in_dim(
        jnp.concatenate([blocks, blocks], axis=0), start, blocks.shape[0], axis=0
    )


def together(*values):
    return lax.optimization_barrier(values)


def local(tokens, norm_gain, gate_weight, up_weight, down_weight):
    x, core = lax.axis_index("x"), lax.axis_index("c")
    gate_t, up_t = gate_weight.T, up_weight.T
    first = [gate_t, shift(gate_t, "c", 1), up_t, shift(up_t, "c", 1)]
    second = [down_weight, shift(down_weight, "c", 1)]
    units = 2 * down_weight.shape[0]
    rows, width = tokens.shape
    part = width // 4

    wide = tokens.astype(F32)
    mean_square = jnp.mean(wide * wide, axis=1, keepdims=True)
    normed = (wide * lax.rsqrt(mean_square + 1e-05) * norm_gain[None, :]).astype(BF16)
    blocks = rolled(normed.reshape(rows, 4, part).transpose(1, 0, 2), x)
    own = jnp.stack(
        [blocks[0]] + [shift(blocks[4 - r], "x", 4 - r) for r in (1, 2, 3)]
    )
    pair = lax.all_gather(own, "c", axis=1, tiled=True)
    near = jnp.concatenate([along_z(pair, 0, -2), along_z(pair, 1, -1)], axis=1)
    far = along_z(near, 2, -2)

    def project(weights, block):
        return lax.dot_general(
            block.reshape(-1, part), weights, (((1,), (1,)), ((), ())), preferred_element_type=F32
        ).reshape(4, -1, 2 * units)

    def exchange(partial):
        return [shift(partial[k].astype(BF16), "x", k) for k in (2, 1, 3)]

    def activate(both, received):
        for value in received:
            both = both + value.astype(F32)
        return (jax.nn.silu(both[:, :units]) * both[:, units:]).astype(BF16)

    def spread(hidden):
        return [shift(hidden, "x", -k) for k in (1, 2, 3)]

    def down(weights, everyone):
        return lax.dot_general(
            jnp.concatenate(everyone, axis=0),
            weights,
            (((1,), (0,)), ((), ())),
            preferred_element_type=F32,
        ).reshape(4, -1, part)

    def sum_over_y(blocks, received):
        return sum((value.astype(F32) for value in received), blocks[0])

    def over_y(value):
        return [shift(value, "y", k) for k in (1, 3, 2)]

    def back_over_y(blocks):
        return [shift(blocks[k].astype(BF16), "y", -k) for k in (1, 3, 2)]

    def by_y(value):
        return [value[:, k * slots : (k + 1) * slots] for k in range(4)]

    slots = near.shape[1]
    near_y = over_y(near)
    *first, down_own, down_other, near_own = together(*first, *second, near)
    second = [down_own, down_other]
    first, far = together(jnp.concatenate(first, axis=0), far)
    far_y = over_y(far)

    first, near_1, near_3, near_2 = together(first, *near_y)
    near_partial = project(first, jnp.concatenate([near_own, near_1, near_2, near_3], axis=1))
    near_sums = exchange(near_partial)
    *second, near_kept = together(*second, near_partial[0])
    second = jnp.concatenate(second, axis=0)

    second, far_1, far_3, far_2 = together(second, *far_y)
    far_partial = project(first, jnp.concatenate([far, far_1, far_2, far_3], axis=1))
    far_sums = exchange(far_partial)
    far_kept, *near_sums = together(far_partial[0], *near_sums)
    near_hidden = activate(near_kept, near_sums)
    near_spread = spread(near_hidden)

    near_hidden, *far_sums = together(near_hidden, *far_sums)
    far_hidden = activate(far_kept, far_sums)
    far_spread = spread(far_hidden)
    far_hidden, *near_spread = together(far_hidden, *near_spread)

    near_down = by_y(down(second, [near_hidden] + near_spread))
    near_back = back_over_y(near_down)
    near_down[0], *far_spread = together(near_down[0], *far_spread)
    far_down = by_y(down(second, [far_hidden] + far_spread))
    far_back = back_over_y(far_down)
    far_down[0], *near_back = together(far_down[0], *near_back)

    near_total = sum_over_y(near_down, near_back)
    half = 2 * rows
    near_pieces = [
        along_z(near_total[:, :half].astype(BF16), 0, 2),
        along_z(near_total[:, half:].astype(BF16), -1, 1),
    ]
    *near_pieces, back_1, back_3, back_2 = together(*near_pieces, *far_back)
    far_total = sum_over_y(far_down, (back_1, back_3, back_2))
    far_pieces = [
        along_z(far_total[:, :half].astype(BF16), -2, 4),
        along_z(far_total[:, half:].astype(BF16), -3, 3),
    ]
    pair = sum(piece.astype(F32) for piece in near_pieces + far_pieces)
    low, high = pair[:, :rows], pair[:, rows:]
    mine = jnp.where(core == 0, low, high)
    other = jnp.where(core == 0, high, low).astype(BF16)
    mine = mine + shift(other, "c", 1).astype(F32)
    columns = [mine[0]] + [shift(mine[k], "x", k) for k in (1, 2, 3)]
    ordered = [columns[0]] * 4
    for k in (1, 2, 3):
        ordered = [
            jnp.where((x - block) % 4 == k, columns[k], value)
            for block, value in enumerate(ordered)
        ]
    return (wide + jnp.concatenate(ordered, axis=1)).astype(BF16)


def solution(mesh):
    torus = Mesh(mesh.devices.reshape(4, 8, 2, 4), ("y", "z", "c", "x"))
    section = ("y", "z", "c")
    return jax.shard_map(
        local,
        mesh=torus,
        in_specs=(
            P(section + ("x",), None),
            P(),
            P("x", section),
            P("x", section),
            P(section, "x"),
        ),
        out_specs=P(section + ("x",), None),
        check_vma=False,
    )
```

```python
import jax
import jax.numpy as jnp
from jax import lax
from jax.sharding import Mesh
from jax.sharding import PartitionSpec as P

F32, BF16 = jnp.float32, jnp.bfloat16
SIZES = {"y": 4, "z": 8, "c": 2, "x": 4}


def shift(value, axis, step):
    n = SIZES[axis]
    return lax.ppermute(value, axis, [(i, (i + step) % n) for i in range(n)])


def along_z(value, first, second):
    steps = (first, second)
    pairs = [
        (2 * z + c, 2 * ((z + steps[c]) % 8) + c) for z in range(8) for c in range(2)
    ]
    return lax.ppermute(value, ("z", "c"), pairs)


def rolled(blocks, start):
    return lax.dynamic_slice_in_dim(
        jnp.concatenate([blocks, blocks], axis=0), start, blocks.shape[0], axis=0
    )


def together(*values):
    return lax.optimization_barrier(values)


def local(tokens, norm_gain, gate_weight, up_weight, down_weight):
    x, core = lax.axis_index("x"), lax.axis_index("c")
    gate_t, up_t = gate_weight.T, up_weight.T
    first = [gate_t, shift(gate_t, "c", 1), up_t, shift(up_t, "c", 1)]
    units = 2 * down_weight.shape[0]
    rows, width = tokens.shape
    part = width // 4

    wide = tokens.astype(F32)
    mean_square = jnp.mean(wide * wide, axis=1, keepdims=True)
    normed = (wide * lax.rsqrt(mean_square + 1e-05) * norm_gain[None, :]).astype(BF16)
    blocks = rolled(normed.reshape(rows, 4, part).transpose(1, 0, 2), x)
    own = jnp.stack(
        [blocks[0]] + [shift(blocks[4 - r], "x", 4 - r) for r in (1, 2, 3)]
    )
    pair = lax.all_gather(own, "c", axis=1, tiled=True)
    near = jnp.concatenate([along_z(pair, 0, -2), along_z(pair, 1, -1)], axis=1)
    far = along_z(near, 2, -2)

    def project(weights, block):
        return lax.dot_general(
            block.reshape(-1, part), weights, (((1,), (1,)), ((), ())), preferred_element_type=F32
        ).reshape(4, -1, 2 * units)

    def exchange(partial):
        return [shift(partial[k].astype(BF16), "x", k) for k in (2, 1, 3)]

    def activate(both, received):
        for value in received:
            both = both + value.astype(F32)
        return (jax.nn.silu(both[:, :units]) * both[:, units:]).astype(BF16)

    def spread(hidden):
        return [shift(hidden, "x", -k) for k in (1, 2, 3)]

    def down(weights, everyone):
        return lax.dot_general(
            jnp.concatenate(everyone, axis=0),
            weights,
            (((1,), (0,)), ((), ())),
            preferred_element_type=F32,
        ).reshape(4, -1, part)

    def sum_over_y(blocks, received):
        return sum((value.astype(F32) for value in received), blocks[0])

    def over_y(value):
        return [shift(value, "y", k) for k in (1, 3, 2)]

    def back_over_y(blocks):
        return [shift(blocks[k].astype(BF16), "y", -k) for k in (1, 3, 2)]

    def by_y(value):
        return [value[:, k * slots : (k + 1) * slots] for k in range(4)]

    slots = near.shape[1]
    near_y = over_y(near)
    *first, down_own, near_own = together(*first, down_weight, near)
    second = [down_own, shift(down_own, "c", 1)]
    first, far = together(jnp.concatenate(first, axis=0), far)
    far_y = over_y(far)

    first, near_1, near_3, near_2 = together(first, *near_y)
    near_partial = project(first, jnp.concatenate([near_own, near_1, near_2, near_3], axis=1))
    near_sums = exchange(near_partial)
    *second, near_kept = together(*second, near_partial[0])
    second = jnp.concatenate(second, axis=0)

    second, far_1, far_3, far_2 = together(second, *far_y)
    far_partial = project(first, jnp.concatenate([far, far_1, far_2, far_3], axis=1))
    far_sums = exchange(far_partial)
    far_kept, *near_sums = together(far_partial[0], *near_sums)
    near_hidden = activate(near_kept, near_sums)
    near_spread = spread(near_hidden)

    near_hidden, *far_sums = together(near_hidden, *far_sums)
    far_hidden = activate(far_kept, far_sums)
    far_spread = spread(far_hidden)
    far_hidden, *near_spread = together(far_hidden, *near_spread)

    near_down = by_y(down(second, [near_hidden] + near_spread))
    near_back = back_over_y(near_down)
    near_down[0], *far_spread = together(near_down[0], *far_spread)
    far_down = by_y(down(second, [far_hidden] + far_spread))
    far_back = back_over_y(far_down)
    far_down[0], *near_back = together(far_down[0], *near_back)

    near_total = sum_over_y(near_down, near_back)
    half = 2 * rows
    near_pieces = [
        along_z(near_total[:, :half].astype(BF16), 0, 2),
        along_z(near_total[:, half:].astype(BF16), -1, 1),
    ]
    *near_pieces, back_1, back_3, back_2 = together(*near_pieces, *far_back)
    far_total = sum_over_y(far_down, (back_1, back_3, back_2))
    far_pieces = [
        along_z(far_total[:, :half].astype(BF16), -2, 4),
        along_z(far_total[:, half:].astype(BF16), -3, 3),
    ]
    pair = sum(piece.astype(F32) for piece in near_pieces + far_pieces)
    low, high = pair[:, :rows], pair[:, rows:]
    mine = jnp.where(core == 0, low, high)
    other = jnp.where(core == 0, high, low).astype(BF16)
    mine = mine + shift(other, "c", 1).astype(F32)
    columns = [mine[0]] + [shift(mine[k], "x", k) for k in (1, 2, 3)]
    ordered = [columns[0]] * 4
    for k in (1, 2, 3):
        ordered = [
            jnp.where((x - block) % 4 == k, columns[k], value)
            for block, value in enumerate(ordered)
        ]
    return (wide + jnp.concatenate(ordered, axis=1)).astype(BF16)


def solution(mesh):
    torus = Mesh(mesh.devices.reshape(4, 8, 2, 4), ("y", "z", "c", "x"))
    section = ("y", "z", "c")
    return jax.shard_map(
        local,
        mesh=torus,
        in_specs=(
            P(section + ("x",), None),
            P(),
            P("x", section),
            P("x", section),
            P(section, "x"),
        ),
        out_specs=P(section + ("x",), None),
        check_vma=False,
    )
```

```python
import jax
import jax.numpy as jnp
from jax import lax
from jax.sharding import Mesh
from jax.sharding import PartitionSpec as P

F32, BF16 = jnp.float32, jnp.bfloat16
SIZES = {"y": 4, "z": 8, "c": 2, "x": 4}


def shift(value, axis, step):
    n = SIZES[axis]
    return lax.ppermute(value, axis, [(i, (i + step) % n) for i in range(n)])


def along_z(value, first, second):
    steps = (first, second)
    pairs = [
        (2 * z + c, 2 * ((z + steps[c]) % 8) + c) for z in range(8) for c in range(2)
    ]
    return lax.ppermute(value, ("z", "c"), pairs)


def rolled(blocks, start):
    return lax.dynamic_slice_in_dim(
        jnp.concatenate([blocks, blocks], axis=0), start, blocks.shape[0], axis=0
    )


def together(*values):
    return lax.optimization_barrier(values)


def local(tokens, norm_gain, gate_weight, up_weight, down_weight):
    x, core = lax.axis_index("x"), lax.axis_index("c")
    gate_t, up_t = gate_weight.T, up_weight.T
    first = [gate_t, shift(gate_t, "c", 1), up_t, shift(up_t, "c", 1)]
    units = 2 * down_weight.shape[0]
    rows, width = tokens.shape
    part = width // 4

    wide = tokens.astype(F32)
    mean_square = jnp.mean(wide * wide, axis=1, keepdims=True)
    normed = (wide * lax.rsqrt(mean_square + 1e-05) * norm_gain[None, :]).astype(BF16)
    blocks = rolled(normed.reshape(rows, 4, part).transpose(1, 0, 2), x)
    own = jnp.stack(
        [blocks[0]] + [shift(blocks[4 - r], "x", 4 - r) for r in (1, 2, 3)]
    )
    pair = lax.all_gather(own, "c", axis=1, tiled=True)
    near = jnp.concatenate([along_z(pair, 0, -2), along_z(pair, 1, -1)], axis=1)
    far = along_z(near, 2, -2)

    def project(weights, block):
        return lax.dot_general(
            block.reshape(-1, part), weights, (((1,), (1,)), ((), ())), preferred_element_type=F32
        ).reshape(4, -1, 2 * units)

    def exchange(partial):
        return [shift(partial[k].astype(BF16), "x", k) for k in (2, 1, 3)]

    def activate(both, received):
        for value in received:
            both = both + value.astype(F32)
        return (jax.nn.silu(both[:, :units]) * both[:, units:]).astype(BF16)

    def spread(hidden):
        return [shift(hidden, "x", -k) for k in (1, 2, 3)]

    def down(weights, everyone):
        return lax.dot_general(
            jnp.concatenate(everyone, axis=0),
            weights,
            (((1,), (0,)), ((), ())),
            preferred_element_type=F32,
        ).reshape(4, -1, part)

    def sum_over_y(blocks, received):
        return sum((value.astype(F32) for value in received), blocks[0])

    def over_y(value):
        return [shift(value, "y", k) for k in (1, 3, 2)]

    def back_over_y(blocks):
        return [shift(blocks[k].astype(BF16), "y", -k) for k in (1, 3, 2)]

    def by_y(value):
        return [value[:, k * slots : (k + 1) * slots] for k in range(4)]

    slots = near.shape[1]
    near_y = over_y(near)
    *first, down_own, near_own = together(*first, down_weight, near)
    second = [down_own, shift(down_own, "c", 1)]
    first, far = together(jnp.concatenate(first, axis=0), far)
    far_y = over_y(far)

    first, near_1, near_3, near_2 = together(first, *near_y)
    near_partial = project(first, jnp.concatenate([near_own, near_1, near_2, near_3], axis=1))
    near_sums = exchange(near_partial)
    *second, near_kept = together(*second, near_partial[0])
    second = jnp.concatenate(second, axis=0)

    second, far_1, far_3, far_2 = together(second, *far_y)
    far_partial = project(first, jnp.concatenate([far, far_1, far_2, far_3], axis=1))
    far_sums = exchange(far_partial)
    far_kept, *near_sums = together(far_partial[0], *near_sums)
    near_hidden = activate(near_kept, near_sums)
    near_spread = spread(near_hidden)
    near_down = by_y(down(second, [near_hidden] + near_spread))
    near_back = back_over_y(near_down)

    near_down[0], *far_sums = together(near_down[0], *far_sums)
    far_hidden = activate(far_kept, far_sums)
    far_spread = spread(far_hidden)
    far_hidden, *near_back = together(far_hidden, *near_back)
    far_down = by_y(down(second, [far_hidden] + far_spread))
    far_back = back_over_y(far_down)

    near_total = sum_over_y(near_down, near_back)
    half = 2 * rows
    near_pieces = [
        along_z(near_total[:, :half].astype(BF16), 0, 2),
        along_z(near_total[:, half:].astype(BF16), -1, 1),
    ]
    *near_pieces, back_1, back_3, back_2 = together(*near_pieces, *far_back)
    far_total = sum_over_y(far_down, (back_1, back_3, back_2))
    low, high = far_total[:, :half], far_total[:, half:]
    passing = along_z(jnp.where(core == 0, high, low).astype(BF16), -1, 1).astype(F32)
    joined = jnp.where(core == 0, low, high) + passing
    far_piece = along_z(joined.astype(BF16), -2, 3)
    pair = sum(piece.astype(F32) for piece in near_pieces + [far_piece])
    low, high = pair[:, :rows], pair[:, rows:]
    mine = jnp.where(core == 0, low, high)
    other = jnp.where(core == 0, high, low).astype(BF16)
    mine = mine + shift(other, "c", 1).astype(F32)
    columns = [mine[0]] + [shift(mine[k], "x", k) for k in (1, 2, 3)]
    ordered = [columns[0]] * 4
    for k in (1, 2, 3):
        ordered = [
            jnp.where((x - block) % 4 == k, columns[k], value)
            for block, value in enumerate(ordered)
        ]
    return (wide + jnp.concatenate(ordered, axis=1)).astype(BF16)


def solution(mesh):
    torus = Mesh(mesh.devices.reshape(4, 8, 2, 4), ("y", "z", "c", "x"))
    section = ("y", "z", "c")
    return jax.shard_map(
        local,
        mesh=torus,
        in_specs=(
            P(section + ("x",), None),
            P(),
            P("x", section),
            P("x", section),
            P(section, "x"),
        ),
        out_specs=P(section + ("x",), None),
        check_vma=False,
    )
```

```python
import jax
import jax.numpy as jnp
from jax import lax
from jax.sharding import Mesh
from jax.sharding import PartitionSpec as P

F32, BF16 = jnp.float32, jnp.bfloat16
SIZES = {"y": 4, "z": 8, "c": 2, "x": 4}


def shift(value, axis, step):
    n = SIZES[axis]
    return lax.ppermute(value, axis, [(i, (i + step) % n) for i in range(n)])


def along_z(value, first, second):
    steps = (first, second)
    pairs = [
        (2 * z + c, 2 * ((z + steps[c]) % 8) + c) for z in range(8) for c in range(2)
    ]
    return lax.ppermute(value, ("z", "c"), pairs)


def rolled(blocks, start):
    return lax.dynamic_slice_in_dim(
        jnp.concatenate([blocks, blocks], axis=0), start, blocks.shape[0], axis=0
    )


def together(*values):
    return lax.optimization_barrier(values)


def local(tokens, norm_gain, gate_weight, up_weight, down_weight):
    x, core = lax.axis_index("x"), lax.axis_index("c")
    gate_t, up_t = gate_weight.T, up_weight.T
    first = [gate_t, shift(gate_t, "c", 1), up_t, shift(up_t, "c", 1)]
    units = 2 * down_weight.shape[0]
    rows, width = tokens.shape
    part = width // 4

    wide = tokens.astype(F32)
    mean_square = jnp.mean(wide * wide, axis=1, keepdims=True)
    normed = (wide * lax.rsqrt(mean_square + 1e-05) * norm_gain[None, :]).astype(BF16)
    blocks = rolled(normed.reshape(rows, 4, part).transpose(1, 0, 2), x)
    own = jnp.stack(
        [blocks[0]] + [shift(blocks[4 - r], "x", 4 - r) for r in (1, 2, 3)]
    )
    pair = lax.all_gather(own, "c", axis=1, tiled=True)
    near = jnp.concatenate([along_z(pair, 0, -2), along_z(pair, 1, -1)], axis=1)
    far = along_z(near, 2, -2)

    def project(weights, block):
        return lax.dot_general(
            block.reshape(-1, part), weights, (((1,), (1,)), ((), ())), preferred_element_type=F32
        ).reshape(4, -1, 2 * units)

    def exchange(partial):
        return [shift(partial[k].astype(BF16), "x", k) for k in (1, 3, 2)]

    def activate(both, received):
        for value in received:
            both = both + value.astype(F32)
        return (jax.nn.silu(both[:, :units]) * both[:, units:]).astype(BF16)

    def spread(hidden):
        one, three, two = (shift(hidden, "x", -k) for k in (1, 3, 2))
        return [one, two, three]

    def down(weights, everyone):
        return lax.dot_general(
            jnp.concatenate(everyone, axis=0),
            weights,
            (((1,), (0,)), ((), ())),
            preferred_element_type=F32,
        ).reshape(4, -1, part)

    def sum_over_y(blocks, received):
        return sum((value.astype(F32) for value in received), blocks[0])

    def over_y(value):
        return [shift(value, "y", k) for k in (1, 3, 2)]

    def back_over_y(blocks):
        return [shift(blocks[k].astype(BF16), "y", -k) for k in (1, 3, 2)]

    def by_y(value):
        return [value[:, k * slots : (k + 1) * slots] for k in range(4)]

    slots = near.shape[1]
    near_y = over_y(near)
    *first, down_own, near_own = together(*first, down_weight, near)
    second = [down_own, shift(down_own, "c", 1)]
    first, far = together(jnp.concatenate(first, axis=0), far)
    far_y = over_y(far)

    first, near_1, near_3, near_2 = together(first, *near_y)
    near_partial = project(first, jnp.concatenate([near_own, near_1, near_2, near_3], axis=1))
    near_sums = exchange(near_partial)
    *second, near_kept = together(*second, near_partial[0])
    second = jnp.concatenate(second, axis=0)

    second, far_1, far_3, far_2 = together(second, *far_y)
    far_partial = project(first, jnp.concatenate([far, far_1, far_2, far_3], axis=1))
    far_sums = exchange(far_partial)
    far_kept, *near_sums = together(far_partial[0], *near_sums)
    near_hidden = activate(near_kept, near_sums)
    near_spread = spread(near_hidden)

    near_hidden, *far_sums = together(near_hidden, *far_sums)
    far_hidden = activate(far_kept, far_sums)
    far_spread = spread(far_hidden)
    far_hidden, *near_spread = together(far_hidden, *near_spread)

    near_down = by_y(down(second, [near_hidden] + near_spread))
    near_back = back_over_y(near_down)
    near_down[0], *far_spread = together(near_down[0], *far_spread)
    far_down = by_y(down(second, [far_hidden] + far_spread))
    far_back = back_over_y(far_down)
    far_down[0], *near_back = together(far_down[0], *near_back)

    near_total = sum_over_y(near_down, near_back)
    half = 2 * rows
    near_pieces = [
        along_z(near_total[:, :half].astype(BF16), 0, 2),
        along_z(near_total[:, half:].astype(BF16), -1, 1),
    ]
    *near_pieces, back_1, back_3, back_2 = together(*near_pieces, *far_back)
    far_total = sum_over_y(far_down, (back_1, back_3, back_2))
    far_pieces = [
        along_z(far_total[:, :half].astype(BF16), -2, 4),
        along_z(far_total[:, half:].astype(BF16), -3, 3),
    ]
    pair = sum(piece.astype(F32) for piece in near_pieces + far_pieces)
    low, high = pair[:, :rows], pair[:, rows:]
    mine = jnp.where(core == 0, low, high)
    other = jnp.where(core == 0, high, low).astype(BF16)
    mine = mine + shift(other, "c", 1).astype(F32)
    columns = [mine[0]] + [shift(mine[k], "x", k) for k in (1, 2, 3)]
    ordered = [columns[0]] * 4
    for k in (1, 2, 3):
        ordered = [
            jnp.where((x - block) % 4 == k, columns[k], value)
            for block, value in enumerate(ordered)
        ]
    return (wide + jnp.concatenate(ordered, axis=1)).astype(BF16)


def solution(mesh):
    torus = Mesh(mesh.devices.reshape(4, 8, 2, 4), ("y", "z", "c", "x"))
    section = ("y", "z", "c")
    return jax.shard_map(
        local,
        mesh=torus,
        in_specs=(
            P(section + ("x",), None),
            P(),
            P("x", section),
            P("x", section),
            P(section, "x"),
        ),
        out_specs=P(section + ("x",), None),
        check_vma=False,
    )
```

```python
import jax
import jax.numpy as jnp
from jax import lax
from jax.sharding import Mesh
from jax.sharding import PartitionSpec as P

F32, BF16 = jnp.float32, jnp.bfloat16
SIZES = {"y": 4, "z": 8, "c": 2, "x": 4}


def shift(value, axis, step):
    n = SIZES[axis]
    return lax.ppermute(value, axis, [(i, (i + step) % n) for i in range(n)])


def along_z(value, first, second):
    steps = (first, second)
    pairs = [
        (2 * z + c, 2 * ((z + steps[c]) % 8) + c) for z in range(8) for c in range(2)
    ]
    return lax.ppermute(value, ("z", "c"), pairs)


def rolled(blocks, start):
    return lax.dynamic_slice_in_dim(
        jnp.concatenate([blocks, blocks], axis=0), start, blocks.shape[0], axis=0
    )


def together(*values):
    return lax.optimization_barrier(values)


def local(tokens, norm_gain, gate_weight, up_weight, down_weight):
    x, core = lax.axis_index("x"), lax.axis_index("c")
    gate_t, up_t = gate_weight.T, up_weight.T
    first = [gate_t, shift(gate_t, "c", 1), up_t, shift(up_t, "c", 1)]
    units = 2 * down_weight.shape[0]
    rows, width = tokens.shape
    part = width // 4

    wide = tokens.astype(F32)
    mean_square = jnp.mean(wide * wide, axis=1, keepdims=True)
    normed = (wide * lax.rsqrt(mean_square + 1e-05) * norm_gain[None, :]).astype(BF16)
    blocks = rolled(normed.reshape(rows, 4, part).transpose(1, 0, 2), x)
    own = jnp.stack(
        [blocks[0]] + [shift(blocks[4 - r], "x", 4 - r) for r in (1, 2, 3)]
    )
    pair = lax.all_gather(own, "c", axis=1, tiled=True)
    near = jnp.concatenate([along_z(pair, 0, -2), along_z(pair, 1, -1)], axis=1)
    far = along_z(near, 2, -2)

    def project(weights, block):
        return lax.dot_general(
            block.reshape(-1, part), weights, (((1,), (1,)), ((), ())), preferred_element_type=F32
        ).reshape(4, -1, 2 * units)

    def exchange(partial):
        return [shift(partial[k].astype(BF16), "x", k) for k in (1, 3, 2)]

    def activate(both, received):
        for value in received:
            both = both + value.astype(F32)
        return (jax.nn.silu(both[:, :units]) * both[:, units:]).astype(BF16)

    def spread(hidden):
        return [shift(hidden, "x", -k) for k in (1, 3, 2)]

    def down(weights, everyone):
        return lax.dot_general(
            jnp.concatenate(everyone, axis=0),
            weights,
            (((1,), (0,)), ((), ())),
            preferred_element_type=F32,
        ).reshape(4, -1, part)

    def sum_over_y(blocks, received):
        return sum((value.astype(F32) for value in received), blocks[0])

    def over_y(value):
        return [shift(value, "y", k) for k in (1, 3, 2)]

    def back_over_y(blocks):
        return [shift(blocks[k].astype(BF16), "y", -k) for k in (1, 3, 2)]

    def by_y(value):
        return [value[:, k * slots : (k + 1) * slots] for k in range(4)]

    slots = near.shape[1]
    near_y = over_y(near)
    *first, down_own, near_own = together(*first, down_weight, near)
    second = [down_own, shift(down_own, "c", 1)]
    first, far = together(jnp.concatenate(first, axis=0), far)
    far_y = over_y(far)

    first, near_1, near_3, near_2 = together(first, *near_y)
    near_partial = project(first, jnp.concatenate([near_own, near_1, near_2, near_3], axis=1))
    near_sums = exchange(near_partial)
    *second, near_kept = together(*second, near_partial[0])
    second = jnp.concatenate(second, axis=0)

    second, far_1, far_3, far_2 = together(second, *far_y)
    far_partial = project(first, jnp.concatenate([far, far_1, far_2, far_3], axis=1))
    far_sums = exchange(far_partial)
    far_kept, *near_sums = together(far_partial[0], *near_sums)
    near_hidden = activate(near_kept, near_sums)
    near_spread = spread(near_hidden)

    near_hidden, *far_sums = together(near_hidden, *far_sums)
    far_hidden = activate(far_kept, far_sums)
    far_spread = spread(far_hidden)
    far_hidden, *near_spread = together(far_hidden, *near_spread)

    near_down = by_y(down(second, [near_hidden] + near_spread))
    near_back = back_over_y(near_down)
    near_down[0], *far_spread = together(near_down[0], *far_spread)
    far_down = by_y(down(second, [far_hidden] + far_spread))
    far_back = back_over_y(far_down)
    far_down[0], *near_back = together(far_down[0], *near_back)

    near_total = sum_over_y(near_down, near_back)
    half = 2 * rows
    near_pieces = [
        along_z(near_total[:, :half].astype(BF16), 0, 2),
        along_z(near_total[:, half:].astype(BF16), -1, 1),
    ]
    *near_pieces, back_1, back_3, back_2 = together(*near_pieces, *far_back)
    far_total = sum_over_y(far_down, (back_1, back_3, back_2))
    far_pieces = [
        along_z(far_total[:, :half].astype(BF16), -2, 4),
        along_z(far_total[:, half:].astype(BF16), -3, 3),
    ]
    pair = sum(piece.astype(F32) for piece in near_pieces + far_pieces)
    low, high = pair[:, :rows], pair[:, rows:]
    mine = jnp.where(core == 0, low, high)
    other = jnp.where(core == 0, high, low).astype(BF16)
    mine = mine + shift(other, "c", 1).astype(F32)
    columns = [mine[0]] + [shift(mine[place], "x", k) for k, place in ((1, 1), (2, 3), (3, 2))]
    ordered = [columns[0]] * 4
    for k in (1, 2, 3):
        ordered = [
            jnp.where((x - block) % 4 == k, columns[k], value)
            for block, value in enumerate(ordered)
        ]
    return (wide + jnp.concatenate(ordered, axis=1)).astype(BF16)


def solution(mesh):
    torus = Mesh(mesh.devices.reshape(4, 8, 2, 4), ("y", "z", "c", "x"))
    section = ("y", "z", "c")
    return jax.shard_map(
        local,
        mesh=torus,
        in_specs=(
            P(section + ("x",), None),
            P(),
            P("x", section),
            P("x", section),
            P(section, "x"),
        ),
        out_specs=P(section + ("x",), None),
        check_vma=False,
    )
```

```python
import jax
import jax.numpy as jnp
from jax import lax
from jax.sharding import Mesh
from jax.sharding import PartitionSpec as P

F32, BF16 = jnp.float32, jnp.bfloat16
SIZES = {"y": 4, "z": 8, "c": 2, "x": 4}


def shift(value, axis, step):
    n = SIZES[axis]
    return lax.ppermute(value, axis, [(i, (i + step) % n) for i in range(n)])


def along_z(value, first, second):
    steps = (first, second)
    pairs = [
        (2 * z + c, 2 * ((z + steps[c]) % 8) + c) for z in range(8) for c in range(2)
    ]
    return lax.ppermute(value, ("z", "c"), pairs)


def rolled(blocks, start):
    return lax.dynamic_slice_in_dim(
        jnp.concatenate([blocks, blocks], axis=0), start, blocks.shape[0], axis=0
    )


def together(*values):
    return lax.optimization_barrier(values)


def local(tokens, norm_gain, gate_weight, up_weight, down_weight):
    x, core = lax.axis_index("x"), lax.axis_index("c")
    gate_t, up_t = gate_weight.T, up_weight.T
    first = [gate_t, shift(gate_t, "c", 1), up_t, shift(up_t, "c", 1)]
    units = 2 * down_weight.shape[0]
    rows, width = tokens.shape
    part = width // 4

    wide = tokens.astype(F32)
    mean_square = jnp.mean(wide * wide, axis=1, keepdims=True)
    normed = (wide * lax.rsqrt(mean_square + 1e-05) * norm_gain[None, :]).astype(BF16)
    blocks = rolled(normed.reshape(rows, 4, part).transpose(1, 0, 2), x)
    own = jnp.stack(
        [blocks[0]] + [shift(blocks[4 - r], "x", 4 - r) for r in (1, 2, 3)]
    )
    pair = lax.all_gather(own, "c", axis=1, tiled=True)
    near = jnp.concatenate([along_z(pair, 0, -2), along_z(pair, 1, -1)], axis=1)
    far = along_z(near, 2, -2)

    def project(weights, block):
        return lax.dot_general(
            block.reshape(-1, part), weights, (((1,), (1,)), ((), ())), preferred_element_type=F32
        ).reshape(4, -1, 2 * units)

    def exchange(partial):
        return [shift(partial[k].astype(BF16), "x", k) for k in (1, 3, 2)]

    def activate(both, received):
        for value in received:
            both = both + value.astype(F32)
        return (jax.nn.silu(both[:, :units]) * both[:, units:]).astype(BF16)

    def spread(hidden):
        one, three, two = (shift(hidden, "x", -k) for k in (1, 3, 2))
        return [one, two, three]

    def down(weights, everyone):
        return lax.dot_general(
            jnp.concatenate(everyone, axis=0),
            weights,
            (((1,), (0,)), ((), ())),
            preferred_element_type=F32,
        ).reshape(4, -1, part)

    def sum_over_y(blocks, received):
        return sum((value.astype(F32) for value in received), blocks[0])

    def over_y(value):
        return [shift(value, "y", k) for k in (1, 3, 2)]

    def back_over_y(blocks):
        return [shift(blocks[k].astype(BF16), "y", -k) for k in (1, 3, 2)]

    def by_y(value):
        return [value[:, k * slots : (k + 1) * slots] for k in range(4)]

    slots = near.shape[1]
    near_y = over_y(near)
    *first, down_own, near_own = together(*first, down_weight, near)
    second = [down_own, shift(down_own, "c", 1)]
    first, far = together(jnp.concatenate(first, axis=0), far)
    far_y = over_y(far)

    first, near_1, near_3, near_2 = together(first, *near_y)
    near_partial = project(first, jnp.concatenate([near_own, near_1, near_2, near_3], axis=1))
    near_sums = exchange(near_partial)
    *second, near_kept = together(*second, near_partial[0])
    second = jnp.concatenate(second, axis=0)

    second, far_1, far_3, far_2 = together(second, *far_y)
    far_partial = project(first, jnp.concatenate([far, far_1, far_2, far_3], axis=1))
    far_sums = exchange(far_partial)
    far_kept, *near_sums = together(far_partial[0], *near_sums)
    near_hidden = activate(near_kept, near_sums)
    near_spread = spread(near_hidden)

    near_hidden, *far_sums = together(near_hidden, *far_sums)
    far_hidden = activate(far_kept, far_sums)
    far_spread = spread(far_hidden)
    far_hidden, *near_spread = together(far_hidden, *near_spread)

    near_down = by_y(down(second, [near_hidden] + near_spread))
    near_back = back_over_y(near_down)
    near_down[0], *far_spread = together(near_down[0], *far_spread)
    far_down = by_y(down(second, [far_hidden] + far_spread))
    far_back = back_over_y(far_down)
    far_down[0], *near_back = together(far_down[0], *near_back)

    near_total = sum_over_y(near_down, near_back)
    half = 2 * rows
    near_pieces = [
        along_z(near_total[:, :half].astype(BF16), 0, 2),
        along_z(near_total[:, half:].astype(BF16), -1, 1),
    ]
    *near_pieces, back_1, back_3, back_2 = together(*near_pieces, *far_back)
    far_total = sum_over_y(far_down, (back_1, back_3, back_2))
    far_pieces = [
        along_z(far_total[:, :half].astype(BF16), -2, 4),
        along_z(far_total[:, half:].astype(BF16), -3, 3),
    ]
    pair = sum(piece.astype(F32) for piece in near_pieces + far_pieces)
    low, high = pair[:, :rows], pair[:, rows:]
    mine = jnp.where(core == 0, low, high)
    other = jnp.where(core == 0, high, low).astype(BF16)
    mine = mine + shift(other, "c", 1).astype(F32)
    columns = [mine[0]] + [shift(mine[k].astype(BF16), "x", k).astype(F32) for k in (1, 2, 3)]
    ordered = [columns[0]] * 4
    for k in (1, 2, 3):
        ordered = [
            jnp.where((x - block) % 4 == k, columns[k], value)
            for block, value in enumerate(ordered)
        ]
    return (wide + jnp.concatenate(ordered, axis=1)).astype(BF16)


def solution(mesh):
    torus = Mesh(mesh.devices.reshape(4, 8, 2, 4), ("y", "z", "c", "x"))
    section = ("y", "z", "c")
    return jax.shard_map(
        local,
        mesh=torus,
        in_specs=(
            P(section + ("x",), None),
            P(),
            P("x", section),
            P("x", section),
            P(section, "x"),
        ),
        out_specs=P(section + ("x",), None),
        check_vma=False,
    )
```
